32 devices in a mesh: groups: 2 (over y), section: 4 (over z), head: 4 (over x, core).
Axes of the slice: x: 2, y: 2, z: 4, core: 2. Of those that a mesh axis runs over, the one named last changes fastest.
Arguments:
- rising: bfloat16 [8, 128, 1024], P(('groups', 'section')), parts along dimension 0, may hold values from -24 to 24
- falling: bfloat16 [8, 128, 1024], P(('groups', 'section')), parts along dimension 0, may hold values from -6 to 6
- stash: bfloat16 [8, 3, 128, 1024], P(('groups', 'section')), parts along dimension 0, may hold values from -24 to 24
- queue: bfloat16 [12, 128, 1024], P('groups'), parts along dimension 0, may hold values from -24 to 24
- order: int32 [12], P('groups'), parts along dimension 0, may hold values from 0 to 5, each once
- buckets: int32 [128, 128], replicated, may hold values from 0 to 31, as said below
- bias_table: float32 [4, 32, 64], P('section', None, 'head'), may hold values from -3 to 260
- gain: float32 [4, 1024], P('section'), may hold values from 0.1 to 1.9
- w_qkv: bfloat16 [4, 1024, 64, 3, 128], P('section', None, 'head'), may hold values from -0.1875 to 0.1875
- w_out: bfloat16 [4, 64, 128, 1024], P('section', 'head'), may hold values from -0.0625 to 0.0625
Outputs:
- rising_out: bfloat16 [8, 128, 1024], P(('groups', 'section')), parts along dimension 0
- falling_out: bfloat16 [8, 128, 1024], P(('groups', 'section')), parts along dimension 0
- table_grad: float32 [8, 32, 64], P(('groups', 'section'), None, 'head'), parts along dimension 0
The draws below stay inside these ranges and needn't reach their ends.
There are 2 independent parts, one for each index of `groups`. The reference program is written for one: setup_inputs(seed, part) draws one part's arguments, and reference() takes and returns one part's arrays. A program takes and returns all parts, laid end to end along the dimension named above; an argument that names none is the same for every part. Nothing has to cross between parts.
Inputs may be any that keep to these rules, and one draw needn't show every extreme that they name: `order`: a permutation of 0 to 5. T5's bidirectional bucket of the key's position minus the query's, 32 buckets, distances of 128 or more in the outermost; positions rise by 1 to 4 from token to token, with one jump of 128 or more.
All inputs are finite; a program needn't handle non-finite values.
Results may differ from the reference program's by a relative error of at most 0.019.
Values may be sent and summed in bfloat16 or wider, within the bound.
A program may use at most 128 MiB of HBM per device.

```python
import math
import jax
import jax.numpy as jnp
from jax import lax

D = 1024
HEADS = 64
HD = 128
NB = 32
MAX_DIST = 128
TOK = 128
TICKS = 3
QUEUE = 6
SECTIONS = 4


bucket_edges = (12, 16, 23, 32, 46, 64, 91)


def scaled_rows(key, shape):
    keys = jax.random.split(key, 3)
    base = jax.random.normal(keys[0], shape, jnp.float32)
    row_scale = jnp.exp(jax.random.uniform(keys[1], shape[:-1] + (1,), jnp.float32, math.log(0.3), math.log(3.0)))
    col_scale = jnp.exp(jax.random.uniform(keys[2], (shape[-1],), jnp.float32, math.log(0.3), math.log(3.0)))
    return jnp.clip(base * row_scale * col_scale, -24.0, 24.0).astype(jnp.bfloat16)


def draw_rising(key, part):
    return scaled_rows(jax.random.fold_in(key, 101), (SECTIONS, TOK, D))


def draw_stash(key, part):
    return scaled_rows(jax.random.fold_in(key, 202), (SECTIONS, TICKS, TOK, D))


def draw_queue(key, part):
    return scaled_rows(jax.random.fold_in(key, 303), (QUEUE, TOK, D))


def draw_buckets(key, part):
    keys = jax.random.split(jax.random.fold_in(key, 404), 2)
    steps_between = jax.random.randint(keys[0], (TOK,), 1, 5, dtype=jnp.int32)
    jump_at = jax.random.randint(keys[1], (), 1, TOK, dtype=jnp.int32)
    token_ids = jnp.arange(TOK, dtype=jnp.int32)
    steps_between = jnp.where(token_ids == jump_at, steps_between + MAX_DIST, steps_between)
    positions = jnp.cumsum(steps_between).astype(jnp.int32)
    offset = positions[:, None] - positions[None, :]
    distance = jnp.abs(offset)
    half = NB // 2
    exact = half // 2
    far = jnp.full(distance.shape, exact, jnp.int32)
    for edge in bucket_edges:
        far = far + (distance >= edge).astype(jnp.int32)
    within = jnp.where(distance < exact, distance, jnp.minimum(far, half - 1))
    return (jnp.where(offset < 0, half, 0) + within).astype(jnp.int32)


def draw_bias_table(key, part):
    keys = jax.random.split(jax.random.fold_in(key, 505), 1)
    table = jnp.clip(jax.random.normal(keys[0], (SECTIONS, NB, HEADS), jnp.float32), -3.0, 3.0)
    return table.astype(jnp.float32)


def block_scale(rng, shape, cuts, low, high):
    level, own = 1.0, jax.random.fold_in(rng, 6)
    for position, parts in cuts:
        draws = jnp.exp(jax.random.uniform(jax.random.fold_in(own, position), (parts,), jnp.float32, low / len(cuts), high / len(cuts)))
        level = level * jnp.repeat(draws, shape[position] // parts).reshape([-1 if axis == position else 1 for axis in range(len(shape))])
    return level


def centred(stream_key, dims, width, bound, cuts=(), kind=jnp.bfloat16):
    factor_of = block_scale(stream_key, dims, cuts, -0.22, 0.18) if cuts else 1.0
    entries = jax.random.normal(stream_key, dims, jnp.float32) * width * factor_of
    return jnp.minimum(jnp.maximum(entries, -bound), bound).astype(kind)


def setup_inputs(seed: int = 0, part: int = 0) -> dict:
    key_list = jax.random.split(jax.random.key(seed), 11)
    part_keys = jax.random.split(jax.random.fold_in(key_list[10], part), 11)
    rising = draw_rising(jax.random.fold_in(jax.random.fold_in(key_list[10], part), 71), part)
    falling = centred(part_keys[1], (SECTIONS, TOK, D), 1.0, 6.0, ((0, 4),))
    stash = draw_stash(jax.random.fold_in(jax.random.fold_in(key_list[10], part), 71), part)
    queue = draw_queue(jax.random.fold_in(jax.random.fold_in(key_list[10], part), 71), part)
    order = jax.random.permutation(part_keys[4], QUEUE).astype(jnp.int32)
    buckets = draw_buckets(jax.random.fold_in(key_list[10], 71), part)
    bias_table = draw_bias_table(jax.random.fold_in(key_list[10], 71), part)
    gain = jnp.clip(1.0 + 0.18 * jax.random.normal(key_list[7], (SECTIONS, D), jnp.float32), 0.1, 1.9)
    w_qkv = centred(key_list[8], (SECTIONS, D, HEADS, 3, HD), D ** -0.5, 0.1875, ((0, 4), (2, 4)))
    w_out = centred(key_list[9], (SECTIONS, HEADS, HD, D), (HEADS * HD) ** -0.5, 0.0625, ((0, 4), (1, 4)))
    return dict(rising=rising, falling=falling, stash=stash, queue=queue, order=order, buckets=buckets, bias_table=bias_table, gain=gain, w_qkv=w_qkv, w_out=w_out)


EPSILON = 1e-06
CONTRACT_LAST = (((1,), (1,)), ((), ()))

def normalize(inputs, gain_row):
    as_float = inputs.astype(jnp.float32)
    inverse = lax.rsqrt(lax.optimization_barrier(jnp.mean(as_float * as_float, axis=-1, keepdims=True)) + EPSILON)
    return ((as_float * inverse * gain_row).astype(jnp.bfloat16), inverse)

def forward_parts(inputs, gain_row, w_in, biases):
    normed, inverse = normalize(inputs, gain_row)
    qkv = jnp.dot(normed, w_in, preferred_element_type=jnp.float32).astype(jnp.bfloat16)
    qkv = qkv.reshape(inputs.shape[0], HEADS, 3, HD)
    queries = qkv[:, :, 0]
    keys_part = qkv[:, :, 1]
    values_part = qkv[:, :, 2]
    scores = jnp.einsum('ihd,jhd->hij', queries.astype(jnp.float32), keys_part.astype(jnp.float32)) * HD ** (-0.5) + biases
    attention_probs = jax.nn.softmax(scores, axis=-1)
    return (inverse, queries, keys_part, values_part, attention_probs, attention_probs.astype(jnp.bfloat16))

def section_forward(inputs, gain_row, w_in, w_back, biases):
    inverse, queries, keys_part, values_part, attention_probs, probs_half = forward_parts(inputs, gain_row, w_in, biases)
    attended = jnp.einsum('hij,jhd->ihd', probs_half.astype(jnp.float32), values_part.astype(jnp.float32))
    attended = attended.astype(jnp.bfloat16).reshape(inputs.shape[0], HEADS * HD)
    projected = jnp.dot(attended, w_back, preferred_element_type=jnp.float32)
    return (inputs.astype(jnp.float32) + projected).astype(jnp.bfloat16)

def section_backward(inputs, cotangent, gain_row, w_in, w_back, biases):
    inverse, queries, keys_part, values_part, attention_probs, probs_half = forward_parts(inputs, gain_row, w_in, biases)
    tokens = inputs.shape[0]
    grad_attn = lax.dot_general(cotangent, w_back, CONTRACT_LAST, preferred_element_type=jnp.float32)
    grad_attn = grad_attn.astype(jnp.bfloat16).reshape(tokens, HEADS, HD).astype(jnp.float32)
    grad_probs = jnp.einsum('ihd,jhd->hij', grad_attn, values_part.astype(jnp.float32))
    grad_value = jnp.einsum('hij,ihd->jhd', probs_half.astype(jnp.float32), grad_attn).astype(jnp.bfloat16)
    grad_scores = attention_probs * (grad_probs - lax.optimization_barrier(jnp.sum(attention_probs * grad_probs, axis=-1, keepdims=True)))
    scores_half = grad_scores.astype(jnp.bfloat16).astype(jnp.float32)
    grad_query = (jnp.einsum('hij,jhd->ihd', scores_half, keys_part.astype(jnp.float32)) * HD ** (-0.5)).astype(jnp.bfloat16)
    grad_key = (jnp.einsum('hij,ihd->jhd', scores_half, queries.astype(jnp.float32)) * HD ** (-0.5)).astype(jnp.bfloat16)
    stacked = jnp.stack([grad_query, grad_key, grad_value], axis=2).reshape(tokens, HEADS * 3 * HD)
    grad_normed = lax.dot_general(stacked, w_in, CONTRACT_LAST, preferred_element_type=jnp.float32)
    as_float = inputs.astype(jnp.float32)
    weighted = gain_row * grad_normed
    cubed = inverse * inverse * inverse
    result = cotangent.astype(jnp.float32) + inverse * weighted - as_float * cubed * lax.optimization_barrier(jnp.mean(as_float * weighted, axis=-1, keepdims=True))
    return (result.astype(jnp.bfloat16), grad_scores)

def reference(rising, falling, stash, queue, order, buckets, bias_table, gain, w_qkv, w_out):
    hbias = jnp.transpose(bias_table[:, buckets, :], (0, 3, 1, 2))
    w_in_all = w_qkv.reshape(SECTIONS, D, HEADS * 3 * HD)
    w_back_all = w_out.reshape(SECTIONS, HEADS * HD, D)
    upward = rising
    downward = falling
    accum = jnp.zeros((SECTIONS, HEADS, TOK, TOK), jnp.float32)

    def one_section(packed):
        arriving, kept_rows, cotangent, gain_row, w_in, w_back, biases = packed
        lifted = section_forward(arriving, gain_row, w_in, w_back, biases)
        lowered, grad_scores = section_backward(kept_rows, cotangent, gain_row, w_in, w_back, biases)
        return (lifted, lowered, grad_scores)
    out_up = upward
    out_down = downward
    for tick_index in range(TICKS):
        kept = stash[:, tick_index]
        out_up, out_down, grad_scores = lax.map(one_section, (upward, kept, downward, gain, w_in_all, w_back_all, hbias))
        accum = accum + grad_scores
        if tick_index + 1 < TICKS:
            arrival = queue[order[tick_index]]
            upward = jnp.concatenate([arrival[None], out_up[:-1]], axis=0)
            downward = jnp.concatenate([out_down[1:], out_up[-1:]], axis=0)

    def fold_table(section_accum):
        flat = section_accum.reshape(HEADS, TOK * TOK).T
        return jax.ops.segment_sum(flat, buckets.reshape(-1), num_segments=NB)
    table_grad = lax.map(fold_table, accum)
    return (out_up, out_down, table_grad)
```

```python
import functools

import jax
import jax.numpy as jnp
from jax import lax
from jax.experimental import pallas as pl
from jax.experimental.pallas import tpu as pltpu
from jax.sharding import PartitionSpec as P

EPSILON = 1e-06
MESH = pl.DeviceIdType.MESH
NN = (((1,), (0,)), ((), ()))
NT = (((1,), (1,)), ((), ()))
TN = (((0,), (0,)), ((), ()))


def mm(a, b, dims):
    return lax.dot_general(a, b, dims, preferred_element_type=jnp.float32)


def inverse_rms(x):
    return lax.rsqrt(jnp.mean(x * x, axis=-1, keepdims=True) + EPSILON)


def probabilities(q, k, bias, scale):
    scores = mm(q, k, NT) * scale + bias
    top = jnp.max(scores, axis=-1, keepdims=True)
    raised = jnp.exp(scores - top)
    return raised / jnp.sum(raised, axis=-1, keepdims=True)


def tick_kernel(
    first, pair, head_dim, up_ref, kept_ref, down_ref, gain_ref, wq_ref, wk_ref, wv_ref,
    wo_ref, bias_ref, *rest
):
    if first:
        part_ref, total_ref, normed, acc = rest
        total_in = None
    else:
        total_in, part_ref, total_ref, normed, acc = rest
    step = pl.program_id(0)
    rows = up_ref.shape[0]
    scale = head_dim ** (-0.5)

    @pl.when(step == 0)
    def _():
        for place, source in ((0, up_ref), (1, kept_ref)):
            x = source[...].astype(jnp.float32)
            normed[place * rows : (place + 1) * rows, :] = (
                x * inverse_rms(x) * gain_ref[...]
            ).astype(jnp.bfloat16)
        acc[...] = jnp.zeros_like(acc)

    weights = (wq_ref, wk_ref, wv_ref)
    qkv = [mm(normed[...], w[...], NN).astype(jnp.bfloat16) for w in weights]
    grad_flat = mm(down_ref[...], wo_ref[...], NT).astype(jnp.bfloat16)
    attended, stacked = [], []
    for head in range(pair):
        columns = slice(head * head_dim, (head + 1) * head_dim)
        q, k, v = (part[:, columns] for part in qkv)
        bias = bias_ref[head]
        probs = probabilities(q[:rows], k[:rows], bias, scale).astype(jnp.bfloat16)
        attended.append(mm(probs, v[:rows], NN).astype(jnp.bfloat16))
        q, k, v = q[rows:], k[rows:], v[rows:]
        g = grad_flat[:, columns]
        probs = probabilities(q, k, bias, scale)
        grad_probs = mm(g, v, NT)
        grad_value = mm(probs.astype(jnp.bfloat16), g, TN).astype(jnp.bfloat16)
        grad_scores = probs * (
            grad_probs - jnp.sum(probs * grad_probs, axis=-1, keepdims=True)
        )
        half = grad_scores.astype(jnp.bfloat16)
        grad_query = (mm(half, k, NN) * scale).astype(jnp.bfloat16)
        grad_key = (mm(half, q, TN) * scale).astype(jnp.bfloat16)
        stacked.append((grad_query, grad_key, grad_value))
        if first:
            total_ref[head] = grad_scores
        else:
            total_ref[head] = total_in[head] + grad_scores
    acc[0] += mm(jnp.concatenate(attended, axis=1), wo_ref[...], NN)
    back = [mm(jnp.concatenate(g, axis=1), w[...], NT) for g, w in zip(zip(*stacked), weights)]
    acc[1] += back[0] + back[1] + back[2]

    @pl.when(step == pl.num_programs(0) - 1)
    def _():
        part_ref[...] = acc[...].astype(jnp.bfloat16)


def run_tick(first, up, kept, down, gain, w_in, w_back, biases, total, head_dim):
    heads, rows, _ = biases.shape
    width = up.shape[1]
    pair = 2 if heads % 2 == 0 else 1
    whole = lambda shape: pl.BlockSpec(shape, lambda i: (0,) * len(shape))
    score_spec = pl.BlockSpec((pair, rows, rows), lambda i: (i, 0, 0))
    steps = heads // pair
    weight_spec = lambda c: pl.BlockSpec((width, pair * head_dim), lambda i: (0, c * steps + i))
    in_specs = [
        whole((rows, width)),
        whole((rows, width)),
        whole((rows, width)),
        whole((1, width)),
        weight_spec(0),
        weight_spec(1),
        weight_spec(2),
        pl.BlockSpec((pair * head_dim, width), lambda i: (i, 0)),
        score_spec,
    ]
    operands = [up, kept, down, gain, w_in, w_in, w_in, w_back, biases]
    if not first:
        in_specs.append(score_spec)
        operands.append(total)
    return pl.pallas_call(
        functools.partial(tick_kernel, first, pair, head_dim),
        grid=(steps,),
        in_specs=in_specs,
        out_specs=[whole((2, rows, width)), score_spec],
        out_shape=[
            jax.ShapeDtypeStruct((2, rows, width), jnp.bfloat16),
            jax.ShapeDtypeStruct((heads, rows, rows), jnp.float32),
        ],
        scratch_shapes=[
            pltpu.VMEM((2 * rows, width), jnp.bfloat16),
            pltpu.VMEM((2, rows, width), jnp.float32),
        ],
        compiler_params=pltpu.CompilerParams(vmem_limit_bytes=58 << 20),
    )(*operands)


def link_kernel(
    final, chips, sections, part, up, kept, down, arrival, gain, out_ref,
    near, away, far, share, near_send, near_recv, far_send, far_recv,
    lift_send, lift_recv, gather_send, gather_recv, pass_send, pass_recv,
):
    section = lax.axis_index("section")
    head = lax.axis_index("head")
    chip, core = head // 2, lax.rem(head, 2)
    twin = chip * 2 + (1 - core)

    def peer(k):
        return lax.rem(chip + k, chips)

    barrier = pltpu.get_barrier_semaphore()
    greeted = [twin] + [peer(k) * 2 + core for k in range(1, chips)]
    for other in greeted:
        pl.semaphore_signal(barrier, inc=1, device_id={"head": other}, device_id_type=MESH)
    if not final:
        @pl.when(section > 0)
        def _():
            pl.semaphore_signal(
                barrier, inc=1, device_id={"section": section - 1}, device_id_type=MESH
            )

        @pl.when(section < sections - 1)
        def _():
            pl.semaphore_signal(
                barrier, inc=1, device_id={"section": section + 1}, device_id_type=MESH
            )

    arrivals = len(greeted)
    if not final:
        arrivals = (
            arrivals
            + (section > 0).astype(jnp.int32)
            + (section < sections - 1).astype(jnp.int32)
        )
    pl.semaphore_wait(barrier, arrivals)

    order = list(range(1, chips)) + [0]
    near_copies = {}
    for k in order:
        near_copies[k] = pltpu.make_async_remote_copy(
            src_ref=part.at[:, peer(k), 1 - core],
            dst_ref=near.at[k],
            send_sem=near_send.at[k],
            recv_sem=near_recv.at[k],
            device_id={"head": twin},
            device_id_type=MESH,
        )
        near_copies[k].start()
    far_copies = []
    for k in range(1, chips):
        near_copies[k].wait_recv()
        away[k - 1] = (
            part[:, peer(k), core].astype(jnp.float32) + near[k].astype(jnp.float32)
        ).astype(jnp.bfloat16)
        copy = pltpu.make_async_remote_copy(
            src_ref=away.at[k - 1],
            dst_ref=far.at[k - 1],
            send_sem=far_send.at[k - 1],
            recv_sem=far_recv.at[k - 1],
            device_id={"head": peer(k) * 2 + core},
            device_id_type=MESH,
        )
        copy.start()
        far_copies.append(copy)
    near_copies[0].wait_recv()
    own = part[:, chip, core].astype(jnp.float32) + near[0].astype(jnp.float32)
    as_float = kept[chip, core].astype(jnp.float32)
    inverse = inverse_rms(as_float)
    cubed = inverse * inverse * inverse
    for k in range(chips - 1):
        far_copies[k].wait_recv()
        own = own + far[k].astype(jnp.float32)
    lifted = (up[chip, core].astype(jnp.float32) + own[0]).astype(jnp.bfloat16)
    weighted = gain[...] * own[1]
    lowered = (
        down[chip, core].astype(jnp.float32)
        + inverse * weighted
        - as_float * cubed * jnp.mean(as_float * weighted, axis=-1, keepdims=True)
    ).astype(jnp.bfloat16)

    if final:
        out_ref[0, chip, core] = lifted
        out_ref[1, chip, core] = lowered
    else:
        share[0] = lifted
        share[1] = lowered

        def lift(which, target):
            return pltpu.make_async_remote_copy(
                src_ref=share.at[which],
                dst_ref=out_ref.at[which, chip, core],
                send_sem=lift_send.at[which],
                recv_sem=lift_recv.at[which],
                device_id={"section": target},
                device_id_type=MESH,
            )

        @pl.when(section < sections - 1)
        def _():
            lift(0, section + 1).start()

        @pl.when(section > 0)
        def _():
            lift(1, section - 1).start()

        @pl.when(section == 0)
        def _():
            out_ref[0, chip, core] = arrival[chip, core]

        @pl.when(section == sections - 1)
        def _():
            out_ref[1, chip, core] = lifted

        @pl.when(section > 0)
        def _():
            lift(0, section - 1).wait_recv()

        @pl.when(section < sections - 1)
        def _():
            lift(1, section + 1).wait_recv()

    gathers = []
    for k in range(1, chips):
        copy = pltpu.make_async_remote_copy(
            src_ref=out_ref.at[:, chip, core],
            dst_ref=out_ref.at[:, chip, core],
            send_sem=gather_send.at[k - 1],
            recv_sem=gather_recv.at[k - 1],
            device_id={"head": peer(k) * 2 + core},
            device_id_type=MESH,
        )
        copy.start()
        gathers.append(copy)

    def passing(k):
        source = lax.rem(chip - k + chips, chips)
        return pltpu.make_async_remote_copy(
            src_ref=out_ref.at[:, source, core],
            dst_ref=out_ref.at[:, source, core],
            send_sem=pass_send.at[k],
            recv_sem=pass_recv.at[k],
            device_id={"head": twin},
            device_id_type=MESH,
        )

    passed = [passing(0)]
    passed[0].start()
    for k in range(1, chips):
        gathers[k - 1].wait_recv()
        copy = passing(k)
        copy.start()
        passed.append(copy)
    for copy in passed:
        copy.wait_recv()
    for copy in list(near_copies.values()) + far_copies + gathers + passed:
        copy.wait_send()
    if not final:
        @pl.when(section < sections - 1)
        def _():
            lift(0, section + 1).wait_send()

        @pl.when(section > 0)
        def _():
            lift(1, section - 1).wait_send()


def run_link(final, part, up, kept, down, arrival, gain, sections, heads):
    rows, width = up.shape
    chips, share = heads // 2, rows // heads
    split = lambda a: a.reshape(a.shape[:-2] + (chips, 2, share, width))
    vmem = pl.BlockSpec(memory_space=pltpu.VMEM)
    dma = lambda n: pltpu.SemaphoreType.DMA((n,))
    others = max(chips - 1, 1)
    out = pl.pallas_call(
        functools.partial(link_kernel, final, chips, sections),
        in_specs=[vmem] * 6,
        out_specs=vmem,
        out_shape=jax.ShapeDtypeStruct((2, chips, 2, share, width), jnp.bfloat16),
        scratch_shapes=[
            pltpu.VMEM((chips, 2, share, width), jnp.bfloat16),
            pltpu.VMEM((others, 2, share, width), jnp.bfloat16),
            pltpu.VMEM((others, 2, share, width), jnp.bfloat16),
            pltpu.VMEM((2, share, width), jnp.bfloat16),
            dma(chips), dma(chips), dma(others), dma(others),
            dma(2), dma(2), dma(others), dma(others), dma(chips), dma(chips),
        ],
        compiler_params=pltpu.CompilerParams(
            collective_id=1 if final else 0,
            has_side_effects=True,
            vmem_limit_bytes=16 << 20,
        ),
    )(split(part), split(up), split(kept), split(down), split(arrival), gain)
    return out.reshape(2, rows, width)


def per_device(rising, falling, stash, queue, order, buckets, bias_table, gain, w_qkv, w_out):
    sections = lax.axis_size("section")
    head_count = lax.axis_size("head")
    ticks = stash.shape[1]
    width = rising.shape[2]
    heads_here, head_dim = w_qkv.shape[2], w_qkv.shape[4]
    w_in = jnp.swapaxes(w_qkv[0], 1, 2).reshape(width, 3 * heads_here * head_dim)
    w_back = w_out[0].reshape(heads_here * head_dim, width)
    bucket_ids = jnp.arange(bias_table.shape[1], dtype=jnp.int32)
    onehot = (buckets[None, :, :] == bucket_ids[:, None, None]).astype(jnp.float32)
    biases = jnp.einsum("bij,bh->hij", onehot, bias_table[0], precision=lax.Precision.HIGHEST)
    up, down, total = rising[0], falling[0], None
    for tick in range(ticks):
        final = tick + 1 == ticks
        kept = stash[0, tick]
        part, total = run_tick(
            tick == 0, up, kept, down, gain, w_in, w_back, biases, total, head_dim
        )
        arrival = up if final else lax.dynamic_index_in_dim(queue, order[tick], 0, keepdims=False)
        moved = run_link(final, part, up, kept, down, arrival, gain, sections, head_count)
        up, down = moved[0], moved[1]
    table_grad = jnp.einsum("bij,hij->bh", onehot, total, precision=lax.Precision.HIGHEST)
    return (up[None], down[None], table_grad[None])


def solution(mesh):
    return jax.shard_map(
        per_device,
        mesh=mesh,
        in_specs=(
            P(("groups", "section"), None, None),
            P(("groups", "section"), None, None),
            P(("groups", "section"), None, None, None),
            P("groups", None, None),
            P("groups"),
            P(),
            P("section", None, "head"),
            P("section", None),
            P("section", None, "head", None, None),
            P("section", "head", None, None),
        ),
        out_specs=(
            P(("groups", "section"), None, None),
            P(("groups", "section"), None, None),
            P(("groups", "section"), None, "head"),
        ),
        check_vma=False,
    )
```

```python
import functools

import jax
import jax.numpy as jnp
from jax import lax
from jax.experimental import pallas as pl
from jax.experimental.pallas import tpu as pltpu
from jax.sharding import PartitionSpec as P

EPSILON = 1e-06
MESH = pl.DeviceIdType.MESH
NN = (((1,), (0,)), ((), ()))
NT = (((1,), (1,)), ((), ()))
TN = (((0,), (0,)), ((), ()))


def mm(a, b, dims):
    return lax.dot_general(a, b, dims, preferred_element_type=jnp.float32)


def inverse_rms(x):
    return lax.rsqrt(jnp.mean(x * x, axis=-1, keepdims=True) + EPSILON)


def probabilities(q, k, bias, scale):
    scores = mm(q, k, NT) * scale + bias
    top = jnp.max(scores, axis=-1, keepdims=True)
    raised = jnp.exp(scores - top)
    return raised / jnp.sum(raised, axis=-1, keepdims=True)


def wave_kernel(
    ticks, steps, pair, head_dim, chips, sections,
    order, rising, falling, stash, queue, gain, bias, w_hbm, wo_hbm,
    out_up, out_down, total,
    w, wo, normed, flat_down, acc, cur, part, near, away, far, share,
    w_sem, near_send, near_recv, far_send, far_recv,
    lift_send, lift_recv, gather_send, gather_recv, pass_send, pass_recv,
):
    tick, phase, step = pl.program_id(0), pl.program_id(1), pl.program_id(2)
    section = lax.axis_index("section")
    head = lax.axis_index("head")
    chip, core = head // 2, lax.rem(head, 2)
    twin = chip * 2 + (1 - core)
    rows, width = flat_down.shape
    scale = head_dim ** (-0.5)
    span = pair * head_dim

    def peer(k):
        return lax.rem(chip + k, chips)

    def remote(src, dst, send, recv, target):
        return pltpu.make_async_remote_copy(
            src_ref=src, dst_ref=dst, send_sem=send, recv_sem=recv,
            device_id=target, device_id_type=MESH,
        )

    def flat(x):
        return x.astype(jnp.float32).reshape(rows, width)

    def load(j, c):
        if c < 3:
            source = w_hbm.at[:, pl.ds((c * steps + j) * span, span)]
            return pltpu.make_async_copy(source, w.at[j, c], w_sem.at[j, c])
        return pltpu.make_async_copy(wo_hbm.at[pl.ds(j * span, span)], wo.at[j], w_sem.at[j, 3])

    def near_copy(which, t, k):
        return remote(
            part.at[which, t, peer(k), 1 - core], near.at[which, t, k],
            near_send.at[which, t, k], near_recv.at[which, t, k], {"head": twin},
        )

    def far_copy(which, t, k):
        return remote(
            away.at[which, t, k - 1], far.at[which, t, k - 1],
            far_send.at[which, t, k - 1], far_recv.at[which, t, k - 1],
            {"head": peer(k) * 2 + core},
        )

    def lift_copy(which, t, target):
        return remote(
            share.at[which, t], cur.at[which, t + 1, chip, core],
            lift_send.at[which, t], lift_recv.at[which, t], {"section": target},
        )

    def gather_copy(which, t, k):
        rows_here = cur.at[which, t + 1, chip, core]
        return remote(
            rows_here, rows_here,
            gather_send.at[which, t, k - 1], gather_recv.at[which, t, k - 1],
            {"head": peer(k) * 2 + core},
        )

    def pass_copy(which, t, k):
        rows_here = cur.at[which, t + 1, lax.rem(chip - k + chips, chips), core]
        return remote(
            rows_here, rows_here,
            pass_send.at[which, t, k], pass_recv.at[which, t, k], {"head": twin},
        )

    def begin(which, t):
        part[which, t] = acc[...].reshape(part.shape[2:]).astype(jnp.bfloat16)
        for k in list(range(1, chips)) + [0]:
            near_copy(which, t, k).start()

    def fold(which, t):
        for k in range(1, chips):
            near_copy(which, t, k).wait_recv()
            away[which, t, k - 1] = (
                part[which, t, peer(k), core].astype(jnp.float32)
                + near[which, t, k].astype(jnp.float32)
            ).astype(jnp.bfloat16)
            far_copy(which, t, k).start()

    def ends(which):
        if which == 0:
            return section < sections - 1, section + 1, section > 0, section - 1
        return section > 0, section - 1, section < sections - 1, section + 1

    def finish(which, t):
        near_copy(which, t, 0).wait_recv()
        own = part[which, t, chip, core].astype(jnp.float32) + near[which, t, 0].astype(
            jnp.float32
        )
        for k in range(1, chips):
            far_copy(which, t, k).wait_recv()
            own = own + far[which, t, k - 1].astype(jnp.float32)
        before = cur[which, t, chip, core].astype(jnp.float32)
        if which == 0:
            result = before + own
        else:
            x = stash[t, chip, core].astype(jnp.float32)
            inverse = inverse_rms(x)
            cubed = inverse * inverse * inverse
            weighted = gain[...] * own
            result = (
                before
                + inverse * weighted
                - x * cubed * jnp.mean(x * weighted, axis=-1, keepdims=True)
            )
        share[which, t] = result.astype(jnp.bfloat16)
        sends, target, receives, _ = ends(which)

        @pl.when(t == ticks - 1)
        def _():
            cur[which, t + 1, chip, core] = result.astype(jnp.bfloat16)

        @pl.when((t < ticks - 1) & sends)
        def _():
            lift_copy(which, t, target).start()

        @pl.when((t < ticks - 1) & jnp.logical_not(receives))
        def _():
            if which == 0:
                cur[which, t + 1, chip, core] = queue[order[t], chip, core]
            else:
                cur[which, t + 1, chip, core] = share[0, t]

    def spread(which, t):
        sends, target, receives, source = ends(which)

        @pl.when((t < ticks - 1) & receives)
        def _():
            lift_copy(which, t, source).wait_recv()

        for k in range(1, chips):
            gather_copy(which, t, k).start()
        pass_copy(which, t, 0).start()

    def relay(which, t):
        for k in range(1, chips):
            gather_copy(which, t, k).wait_recv()
            pass_copy(which, t, k).start()

    def settle(which, t):
        sends, target, receives, source = ends(which)
        for k in range(chips):
            pass_copy(which, t, k).wait_recv()
        for k in range(chips):
            near_copy(which, t, k).wait_send()
            pass_copy(which, t, k).wait_send()
        for k in range(1, chips):
            far_copy(which, t, k).wait_send()
            gather_copy(which, t, k).wait_send()

        @pl.when((t < ticks - 1) & sends)
        def _():
            lift_copy(which, t, target).wait_send()

    stages = ((fold, 2), (finish, 4), (spread, 6), (relay, 7))

    def normalize(x):
        normed[...] = (x * inverse_rms(x) * gain[...]).astype(jnp.bfloat16)

    @pl.when((tick == 0) & (phase == 0) & (step == 0))
    def _():
        for j in range(steps):
            for c in range(4):
                load(j, c).start()
        barrier = pltpu.get_barrier_semaphore()
        greeted = [twin] + [peer(k) * 2 + core for k in range(1, chips)]
        for other in greeted:
            pl.semaphore_signal(barrier, inc=1, device_id={"head": other}, device_id_type=MESH)

        @pl.when(section > 0)
        def _():
            pl.semaphore_signal(
                barrier, inc=1, device_id={"section": section - 1}, device_id_type=MESH
            )

        @pl.when(section < sections - 1)
        def _():
            pl.semaphore_signal(
                barrier, inc=1, device_id={"section": section + 1}, device_id_type=MESH
            )

        cur[0, 0] = rising[...]
        cur[1, 0] = falling[...]
        flat_down[...] = flat(falling[...]).astype(jnp.bfloat16)
        total[...] = jnp.zeros_like(total)
        pl.semaphore_wait(
            barrier,
            len(greeted)
            + (section > 0).astype(jnp.int32)
            + (section < sections - 1).astype(jnp.int32),
        )

    @pl.when(phase == 0)
    def _():
        @pl.when(step == 0)
        def _():
            @pl.when(tick > 0)
            def _():
                settle(0, tick - 1)

            normalize(flat(cur[0, tick]))
            acc[...] = jnp.zeros_like(acc)

        @pl.when(tick == 0)
        def _():
            for c in range(4):
                load(step, c).wait()

        for stage, at in stages:
            @pl.when((tick > 0) & (step == at * steps // 8))
            def _(stage=stage):
                stage(1, tick - 1)

        qkv = [mm(normed[...], w[step, c], NN).astype(jnp.bfloat16) for c in range(3)]
        attended = []
        for h in range(pair):
            q, k, v = (a[:, h * head_dim : (h + 1) * head_dim] for a in qkv)
            probs = probabilities(q, k, bias[step * pair + h], scale).astype(jnp.bfloat16)
            attended.append(mm(probs, v, NN).astype(jnp.bfloat16))
        acc[...] += mm(jnp.concatenate(attended, axis=1), wo[step], NN)

        @pl.when(step == steps - 1)
        def _():
            begin(0, tick)

    @pl.when(phase == 1)
    def _():
        @pl.when(step == 0)
        def _():
            @pl.when(tick > 0)
            def _():
                settle(1, tick - 1)
                flat_down[...] = flat(cur[1, tick]).astype(jnp.bfloat16)

            normalize(flat(stash[tick]))
            acc[...] = jnp.zeros_like(acc)

        for stage, at in stages:
            @pl.when(step == at * steps // 8)
            def _(stage=stage):
                stage(0, tick)

        qkv = [mm(normed[...], w[step, c], NN).astype(jnp.bfloat16) for c in range(3)]
        grad_flat = mm(flat_down[...], wo[step], NT).astype(jnp.bfloat16)
        stacked = []
        for h in range(pair):
            columns = slice(h * head_dim, (h + 1) * head_dim)
            q, k, v = (a[:, columns] for a in qkv)
            g = grad_flat[:, columns]
            probs = probabilities(q, k, bias[step * pair + h], scale)
            grad_probs = mm(g, v, NT)
            grad_value = mm(probs.astype(jnp.bfloat16), g, TN).astype(jnp.bfloat16)
            grad_scores = probs * (
                grad_probs - jnp.sum(probs * grad_probs, axis=-1, keepdims=True)
            )
            half = grad_scores.astype(jnp.bfloat16)
            grad_query = (mm(half, k, NN) * scale).astype(jnp.bfloat16)
            grad_key = (mm(half, q, TN) * scale).astype(jnp.bfloat16)
            stacked.append((grad_query, grad_key, grad_value))
            total[step * pair + h] += grad_scores
        back = [
            mm(jnp.concatenate(g, axis=1), w[step, c], NT) for c, g in enumerate(zip(*stacked))
        ]
        acc[...] += back[0] + back[1] + back[2]

        @pl.when(step == steps - 1)
        def _():
            begin(1, tick)

    @pl.when((tick == ticks - 1) & (phase == 1) & (step == steps - 1))
    def _():
        last = ticks - 1
        settle(0, last)
        for stage, _at in stages:
            stage(1, last)
        out_up[...] = cur[0, ticks]
        settle(1, last)
        out_down[...] = cur[1, ticks]


def per_device(rising, falling, stash, queue, order, buckets, bias_table, gain, w_qkv, w_out):
    sections = lax.axis_size("section")
    head_count = lax.axis_size("head")
    ticks = stash.shape[1]
    rows, width = rising.shape[1:]
    heads, head_dim = w_qkv.shape[2], w_qkv.shape[4]
    chips, part_rows = head_count // 2, rows // head_count
    pair = 2 if heads % 2 == 0 else 1
    steps, span = heads // pair, pair * head_dim
    others = max(chips - 1, 1)
    w_in = jnp.swapaxes(w_qkv[0], 1, 2).reshape(width, 3 * heads * head_dim)
    w_back = w_out[0].reshape(heads * head_dim, width)
    bucket_ids = jnp.arange(bias_table.shape[1], dtype=jnp.int32)
    onehot = (buckets[None, :, :] == bucket_ids[:, None, None]).astype(jnp.float32)
    biases = jnp.einsum("bij,bh->hij", onehot, bias_table[0], precision=lax.Precision.HIGHEST)
    split = lambda a: a.reshape(a.shape[:-2] + (chips, 2, part_rows, width))
    vmem = pl.BlockSpec(memory_space=pltpu.VMEM)
    anywhere = pl.BlockSpec(memory_space=pl.ANY)
    tile = (part_rows, width)
    bf16 = lambda *shape: pltpu.VMEM(shape, jnp.bfloat16)
    dma = lambda *shape: pltpu.SemaphoreType.DMA(shape)
    up, down, total = pl.pallas_call(
        functools.partial(wave_kernel, ticks, steps, pair, head_dim, chips, sections),
        grid=(ticks, 2, steps),
        in_specs=[pl.BlockSpec(memory_space=pltpu.SMEM)] + [vmem] * 6 + [anywhere] * 2,
        out_specs=[vmem] * 3,
        out_shape=[
            jax.ShapeDtypeStruct((chips, 2) + tile, jnp.bfloat16),
            jax.ShapeDtypeStruct((chips, 2) + tile, jnp.bfloat16),
            jax.ShapeDtypeStruct((heads, rows, rows), jnp.float32),
        ],
        scratch_shapes=[
            bf16(steps, 3, width, span),
            bf16(steps, span, width),
            bf16(rows, width),
            bf16(rows, width),
            pltpu.VMEM((rows, width), jnp.float32),
            bf16(2, ticks + 1, chips, 2, *tile),
            bf16(2, ticks, chips, 2, *tile),
            bf16(2, ticks, chips, *tile),
            bf16(2, ticks, others, *tile),
            bf16(2, ticks, others, *tile),
            bf16(2, ticks, *tile),
            dma(steps, 4),
            dma(2, ticks, chips), dma(2, ticks, chips),
            dma(2, ticks, others), dma(2, ticks, others),
            dma(2, ticks), dma(2, ticks),
            dma(2, ticks, others), dma(2, ticks, others),
            dma(2, ticks, chips), dma(2, ticks, chips),
        ],
        compiler_params=pltpu.CompilerParams(
            collective_id=0, has_side_effects=True, vmem_limit_bytes=58 << 20
        ),
    )(
        order, split(rising[0]), split(falling[0]), split(stash[0]), split(queue), gain,
        biases, w_in, w_back,
    )
    table_grad = jnp.einsum("bij,hij->bh", onehot, total, precision=lax.Precision.HIGHEST)
    return (up.reshape(1, rows, width), down.reshape(1, rows, width), table_grad[None])


def solution(mesh):
    return jax.shard_map(
        per_device,
        mesh=mesh,
        in_specs=(
            P(("groups", "section"), None, None),
            P(("groups", "section"), None, None),
            P(("groups", "section"), None, None, None),
            P("groups", None, None),
            P("groups"),
            P(),
            P("section", None, "head"),
            P("section", None),
            P("section", None, "head", None, None),
            P("section", "head", None, None),
        ),
        out_specs=(
            P(("groups", "section"), None, None),
            P(("groups", "section"), None, None),
            P(("groups", "section"), None, "head"),
        ),
        check_vma=False,
    )
```

```python
import functools

import jax
import jax.numpy as jnp
from jax import lax
from jax.experimental import pallas as pl
from jax.experimental.pallas import tpu as pltpu
from jax.sharding import PartitionSpec as P

EPSILON = 1e-06
MESH = pl.DeviceIdType.MESH
NN = (((1,), (0,)), ((), ()))
NT = (((1,), (1,)), ((), ()))
TN = (((0,), (0,)), ((), ()))


def mm(a, b, dims):
    return lax.dot_general(a, b, dims, preferred_element_type=jnp.float32)


def inverse_rms(x):
    return lax.rsqrt(jnp.mean(x * x, axis=-1, keepdims=True) + EPSILON)


def probabilities(q, k, bias, scale):
    scores = mm(q, k, NT) * scale + bias
    top = jnp.max(scores, axis=-1, keepdims=True)
    raised = jnp.exp(scores - top)
    return raised / jnp.sum(raised, axis=-1, keepdims=True)


def wave_kernel(
    ticks, steps, pair, head_dim, chips, sections,
    order, rising, falling, stash, queue, gain, bias, buckets, w_hbm, wo,
    moved, table,
    w, w_sem, normed, saved, flat_down, acc, total, sums, cur, part, near, away, far, share,
    near_send, near_recv, far_send, far_recv,
    lift_send, lift_recv, gather_send, gather_recv, pass_send, pass_recv,
):
    section = lax.axis_index("section")
    head = lax.axis_index("head")
    chip, core = head // 2, lax.rem(head, 2)
    twin = chip * 2 + (1 - core)
    rows, width = flat_down.shape
    scale = head_dim ** (-0.5)
    span = pair * head_dim

    def peer(k):
        return lax.rem(chip + k, chips)

    def remote(src, dst, send, recv, target):
        return pltpu.make_async_remote_copy(
            src_ref=src, dst_ref=dst, send_sem=send, recv_sem=recv,
            device_id=target, device_id_type=MESH,
        )

    def flat(x):
        return x.astype(jnp.float32).reshape(rows, width)

    def in_block(step, c):
        return w[step, c]

    def load(step, c):
        source = w_hbm.at[:, pl.ds(pl.multiple_of((c * steps + step) * span, 128), span)]
        return pltpu.make_async_copy(source, w.at[step, c], w_sem.at[step, c])

    def out_block(step):
        return wo[pl.ds(pl.multiple_of(step * span, 128), span), :]

    def near_copy(which, t, k):
        return remote(
            part.at[which, t, peer(k), 1 - core], near.at[which, t, k],
            near_send.at[which, t, k], near_recv.at[which, t, k], {"head": twin},
        )

    def far_copy(which, t, k):
        return remote(
            away.at[which, t, k - 1], far.at[which, t, k - 1],
            far_send.at[which, t, k - 1], far_recv.at[which, t, k - 1],
            {"head": peer(k) * 2 + core},
        )

    def lift_copy(which, t, target):
        return remote(
            share.at[which, t], cur.at[which, t + 1, chip, core],
            lift_send.at[which, t], lift_recv.at[which, t], {"section": target},
        )

    def gather_copy(which, t, k):
        rows_here = cur.at[which, t + 1, chip, core]
        return remote(
            rows_here, rows_here,
            gather_send.at[which, t, k - 1], gather_recv.at[which, t, k - 1],
            {"head": peer(k) * 2 + core},
        )

    def pass_copy(which, t, k):
        rows_here = cur.at[which, t + 1, lax.rem(chip - k + chips, chips), core]
        return remote(
            rows_here, rows_here,
            pass_send.at[which, t, k], pass_recv.at[which, t, k], {"head": twin},
        )

    def begin(which, t):
        part[which, t] = acc[...].reshape(part.shape[2:]).astype(jnp.bfloat16)
        for k in list(range(1, chips)) + [0]:
            near_copy(which, t, k).start()

    def fold(which, t):
        for k in range(1, chips):
            near_copy(which, t, k).wait_recv()
            away[which, t, k - 1] = (
                part[which, t, peer(k), core].astype(jnp.float32)
                + near[which, t, k].astype(jnp.float32)
            ).astype(jnp.bfloat16)
            far_copy(which, t, k).start()

    def ends(which):
        if which == 0:
            return section < sections - 1, section + 1, section > 0, section - 1
        return section > 0, section - 1, section < sections - 1, section + 1

    def finish(which, t):
        near_copy(which, t, 0).wait_recv()
        own = part[which, t, chip, core].astype(jnp.float32) + near[which, t, 0].astype(
            jnp.float32
        )
        for k in range(1, chips):
            far_copy(which, t, k).wait_recv()
            own = own + far[which, t, k - 1].astype(jnp.float32)
        before = cur[which, t, chip, core].astype(jnp.float32)
        if which == 0:
            result = before + own
        else:
            x = stash[t, chip, core].astype(jnp.float32)
            inverse = inverse_rms(x)
            cubed = inverse * inverse * inverse
            weighted = gain[...] * own
            result = (
                before
                + inverse * weighted
                - x * cubed * jnp.mean(x * weighted, axis=-1, keepdims=True)
            )
        share[which, t] = result.astype(jnp.bfloat16)
        sends, target, receives, _ = ends(which)

        if t == ticks - 1:
            cur[which, t + 1, chip, core] = result.astype(jnp.bfloat16)
            return

        @pl.when(sends)
        def _():
            lift_copy(which, t, target).start()

        @pl.when(jnp.logical_not(receives))
        def _():
            if which == 0:
                cur[which, t + 1, chip, core] = queue[order[t], chip, core]
            else:
                cur[which, t + 1, chip, core] = share[0, t]

    def spread(which, t):
        sends, target, receives, source = ends(which)

        if t < ticks - 1:
            @pl.when(receives)
            def _():
                lift_copy(which, t, source).wait_recv()

        for k in range(1, chips):
            gather_copy(which, t, k).start()
        pass_copy(which, t, 0).start()

    def relay(which, t):
        for k in range(1, chips):
            gather_copy(which, t, k).wait_recv()
            pass_copy(which, t, k).start()

    def settle(which, t):
        sends, target, receives, source = ends(which)
        for k in range(chips):
            pass_copy(which, t, k).wait_recv()
        for k in range(chips):
            near_copy(which, t, k).wait_send()
            pass_copy(which, t, k).wait_send()
        for k in range(1, chips):
            far_copy(which, t, k).wait_send()
            gather_copy(which, t, k).wait_send()

        if t < ticks - 1:
            @pl.when(sends)
            def _():
                lift_copy(which, t, target).wait_send()

    stages = ((fold, 1), (finish, 3), (spread, 5), (relay, 7))

    def normalize(place, x):
        normed[place * rows : (place + 1) * rows, :] = (
            x * inverse_rms(x) * gain[...]
        ).astype(jnp.bfloat16)

    def project(step, count):
        source = normed[: count * rows, :]
        return [mm(source, in_block(step, c), NN).astype(jnp.bfloat16) for c in range(3)]

    def advance(step, which, t):
        for stage, at in stages:
            @pl.when(step == at * steps // 8)
            def _(stage=stage):
                stage(which, t)

    def forward(t):
        def run(step, carry):
            if t > 0:
                advance(step, 1, t - 1)
            if t == 0:
                for c in range(3):
                    load(step, c).wait()
            qkv = project(step, 1 if t > 0 else ticks + 1)
            if t == 0:
                for c in range(3):
                    saved[step, c] = qkv[c][rows:]
            attended = []
            for h in range(pair):
                q, k, v = (a[:rows, h * head_dim : (h + 1) * head_dim] for a in qkv)
                probs = probabilities(q, k, bias[step * pair + h], scale).astype(jnp.bfloat16)
                attended.append(mm(probs, v, NN).astype(jnp.bfloat16))
            acc[...] += mm(jnp.concatenate(attended, axis=1), out_block(step), NN)
            return carry

        lax.fori_loop(0, steps, run, 0)

    def backward(t):
        def run(step, carry):
            advance(step, 0, t)
            grad_flat = mm(flat_down[...], out_block(step), NT).astype(jnp.bfloat16)
            stacked = []
            for h in range(pair):
                columns = slice(h * head_dim, (h + 1) * head_dim)
                q, k, v = (
                    saved[step, c, t * rows : (t + 1) * rows, columns] for c in range(3)
                )
                g = grad_flat[:, columns]
                probs = probabilities(q, k, bias[step * pair + h], scale)
                grad_probs = mm(g, v, NT)
                grad_value = mm(probs.astype(jnp.bfloat16), g, TN).astype(jnp.bfloat16)
                grad_scores = probs * (
                    grad_probs - jnp.sum(probs * grad_probs, axis=-1, keepdims=True)
                )
                half = grad_scores.astype(jnp.bfloat16)
                grad_query = (mm(half, k, NN) * scale).astype(jnp.bfloat16)
                grad_key = (mm(half, q, TN) * scale).astype(jnp.bfloat16)
                stacked.append((grad_query, grad_key, grad_value))
                if t == 0:
                    total[step * pair + h] = grad_scores
                else:
                    total[step * pair + h] += grad_scores
            back = [
                mm(jnp.concatenate(g, axis=1), in_block(step, c), NT)
                for c, g in enumerate(zip(*stacked))
            ]
            acc[...] += back[0] + back[1] + back[2]
            return carry

        lax.fori_loop(0, steps, run, 0)

    def tables(low, high):
        def run(b, carry):
            chosen = buckets[...] == b
            sums[b] = jnp.concatenate(
                [
                    jnp.sum(jnp.where(chosen, total[h], 0.0), axis=0, keepdims=True)
                    for h in range(total.shape[0])
                ],
                axis=0,
            )
            return carry

        lax.fori_loop(low, high, run, 0)

    for step in range(steps):
        for c in range(3):
            load(step, c).start()
    barrier = pltpu.get_barrier_semaphore()
    greeted = [twin] + [peer(k) * 2 + core for k in range(1, chips)]
    for other in greeted:
        pl.semaphore_signal(barrier, inc=1, device_id={"head": other}, device_id_type=MESH)

    @pl.when(section > 0)
    def _():
        pl.semaphore_signal(
            barrier, inc=1, device_id={"section": section - 1}, device_id_type=MESH
        )

    @pl.when(section < sections - 1)
    def _():
        pl.semaphore_signal(
            barrier, inc=1, device_id={"section": section + 1}, device_id_type=MESH
        )

    cur[0, 0] = rising[...]
    cur[1, 0] = falling[...]
    flat_down[...] = flat(falling[...]).astype(jnp.bfloat16)
    normalize(0, flat(rising[...]))
    for t in range(ticks):
        normalize(t + 1, flat(stash[t]))
    pl.semaphore_wait(
        barrier,
        len(greeted)
        + (section > 0).astype(jnp.int32)
        + (section < sections - 1).astype(jnp.int32),
    )
    for t in range(ticks):
        if t > 0:
            settle(0, t - 1)
            normalize(0, flat(cur[0, t]))
        acc[...] = jnp.zeros_like(acc)
        forward(t)
        begin(0, t)
        if t > 0:
            settle(1, t - 1)
            flat_down[...] = flat(cur[1, t]).astype(jnp.bfloat16)
        acc[...] = jnp.zeros_like(acc)
        backward(t)
        begin(1, t)
    last = ticks - 1
    settle(0, last)
    moved[0] = cur[0, ticks]
    count = sums.shape[0]
    for i, (stage, _at) in enumerate(stages):
        tables(i * count // 4, (i + 1) * count // 4)
        stage(1, last)
    table[...] = jnp.sum(sums[...], axis=-1)
    settle(1, last)
    moved[1] = cur[1, ticks]


def per_device(rising, falling, stash, queue, order, buckets, bias_table, gain, w_qkv, w_out):
    sections = lax.axis_size("section")
    head_count = lax.axis_size("head")
    ticks = stash.shape[1]
    rows, width = rising.shape[1:]
    heads, head_dim = w_qkv.shape[2], w_qkv.shape[4]
    chips, part_rows = head_count // 2, rows // head_count
    pair = 2 if heads % 2 == 0 else 1
    steps, span = heads // pair, pair * head_dim
    others = max(chips - 1, 1)
    w_in = jnp.swapaxes(w_qkv[0], 1, 2).reshape(width, 3 * heads * head_dim)
    w_back = w_out[0].reshape(heads * head_dim, width)
    bucket_ids = jnp.arange(bias_table.shape[1], dtype=jnp.int32)
    onehot = (buckets[None, :, :] == bucket_ids[:, None, None]).astype(jnp.float32)
    biases = jnp.einsum("bij,bh->hij", onehot, bias_table[0], precision=lax.Precision.HIGHEST)
    split = lambda a: a.reshape(a.shape[:-2] + (chips, 2, part_rows, width))
    vmem = pl.BlockSpec(memory_space=pltpu.VMEM)
    tile = (part_rows, width)
    bf16 = lambda *shape: pltpu.VMEM(shape, jnp.bfloat16)
    dma = lambda *shape: pltpu.SemaphoreType.DMA(shape)
    moved, table = pl.pallas_call(
        functools.partial(wave_kernel, ticks, steps, pair, head_dim, chips, sections),
        in_specs=[pl.BlockSpec(memory_space=pltpu.SMEM)] + [vmem] * 7 + [pl.BlockSpec(memory_space=pl.ANY), vmem],
        out_specs=[vmem] * 2,
        out_shape=[
            jax.ShapeDtypeStruct((2, chips, 2) + tile, jnp.bfloat16),
            jax.ShapeDtypeStruct((bias_table.shape[1], heads), jnp.float32),
        ],
        scratch_shapes=[
            bf16(steps, 3, width, span),
            dma(steps, 3),
            bf16((ticks + 1) * rows, width),
            bf16(steps, 3, ticks * rows, span),
            bf16(rows, width),
            pltpu.VMEM((rows, width), jnp.float32),
            pltpu.VMEM((heads, rows, rows), jnp.float32),
            pltpu.VMEM((bias_table.shape[1], heads, rows), jnp.float32),
            bf16(2, ticks + 1, chips, 2, *tile),
            bf16(2, ticks, chips, 2, *tile),
            bf16(2, ticks, chips, *tile),
            bf16(2, ticks, others, *tile),
            bf16(2, ticks, others, *tile),
            bf16(2, ticks, *tile),
            dma(2, ticks, chips), dma(2, ticks, chips),
            dma(2, ticks, others), dma(2, ticks, others),
            dma(2, ticks), dma(2, ticks),
            dma(2, ticks, others), dma(2, ticks, others),
            dma(2, ticks, chips), dma(2, ticks, chips),
        ],
        compiler_params=pltpu.CompilerParams(
            collective_id=0, has_side_effects=True, vmem_limit_bytes=40 << 20
        ),
    )(
        order, split(rising[0]), split(falling[0]), split(stash[0]), split(queue), gain,
        biases, buckets, w_in, w_back,
    )
    moved = moved.reshape(2, 1, rows, width)
    return (moved[0], moved[1], table[None])


def solution(mesh):
    return jax.shard_map(
        per_device,
        mesh=mesh,
        in_specs=(
            P(("groups", "section"), None, None),
            P(("groups", "section"), None, None),
            P(("groups", "section"), None, None, None),
            P("groups", None, None),
            P("groups"),
            P(),
            P("section", None, "head"),
            P("section", None),
            P("section", None, "head", None, None),
            P("section", "head", None, None),
        ),
        out_specs=(
            P(("groups", "section"), None, None),
            P(("groups", "section"), None, None),
            P(("groups", "section"), None, "head"),
        ),
        check_vma=False,
    )
```

```python
import functools

import jax
import jax.numpy as jnp
from jax import lax
from jax.experimental import pallas as pl
from jax.experimental.pallas import tpu as pltpu
from jax.sharding import PartitionSpec as P

EPSILON = 1e-06
MESH = pl.DeviceIdType.MESH
NN = (((1,), (0,)), ((), ()))
NT = (((1,), (1,)), ((), ()))
TN = (((0,), (0,)), ((), ()))


def mm(a, b, dims):
    return lax.dot_general(a, b, dims, preferred_element_type=jnp.float32)


def inverse_rms(x):
    return lax.rsqrt(jnp.mean(x * x, axis=-1, keepdims=True) + EPSILON)


def probabilities(q, k, bias, scale):
    scores = mm(q, k, NT) * scale + bias
    top = jnp.max(scores, axis=-1, keepdims=True)
    raised = jnp.exp(scores - top)
    return raised / jnp.sum(raised, axis=-1, keepdims=True)


def wave_kernel(
    ticks, steps, pair, head_dim, chips, sections,
    order, rising, falling, stash, queue, gain, bias, buckets, w_hbm, wo,
    moved, table,
    w, w_sem, normed, saved, flat_down, acc, total, sums, cur, part, near, away, far, share,
    near_send, near_recv, far_send, far_recv,
    lift_send, lift_recv, gather_send, gather_recv, pass_send, pass_recv,
):
    section = lax.axis_index("section")
    head = lax.axis_index("head")
    chip, core = head // 2, lax.rem(head, 2)
    twin = chip * 2 + (1 - core)
    rows, width = flat_down.shape
    scale = head_dim ** (-0.5)
    span = pair * head_dim

    def peer(k):
        return lax.rem(chip + k, chips)

    def remote(src, dst, send, recv, target):
        return pltpu.make_async_remote_copy(
            src_ref=src, dst_ref=dst, send_sem=send, recv_sem=recv,
            device_id=target, device_id_type=MESH,
        )

    def flat(x):
        return x.astype(jnp.float32).reshape(rows, width)

    def in_block(step, c):
        return w[step, c]

    def load(step, c):
        source = w_hbm.at[:, pl.ds(pl.multiple_of((c * steps + step) * span, 128), span)]
        return pltpu.make_async_copy(source, w.at[step, c], w_sem.at[step, c])

    def out_block(step):
        return wo[pl.ds(pl.multiple_of(step * span, 128), span), :]

    def near_copy(which, t, k):
        return remote(
            part.at[which, t, peer(k), 1 - core], near.at[which, t, k],
            near_send.at[which, t, k], near_recv.at[which, t, k], {"head": twin},
        )

    def far_copy(which, t, k):
        return remote(
            away.at[which, t, k - 1], far.at[which, t, k - 1],
            far_send.at[which, t, k - 1], far_recv.at[which, t, k - 1],
            {"head": peer(k) * 2 + core},
        )

    def lift_copy(which, t, target):
        return remote(
            share.at[which, t], cur.at[which, t + 1, chip, core],
            lift_send.at[which, t], lift_recv.at[which, t], {"section": target},
        )

    def gather_copy(which, t, k):
        rows_here = cur.at[which, t + 1, chip, core]
        return remote(
            rows_here, rows_here,
            gather_send.at[which, t, k - 1], gather_recv.at[which, t, k - 1],
            {"head": peer(k) * 2 + core},
        )

    def pass_copy(which, t, k):
        rows_here = cur.at[which, t + 1, lax.rem(chip - k + chips, chips), core]
        return remote(
            rows_here, rows_here,
            pass_send.at[which, t, k], pass_recv.at[which, t, k], {"head": twin},
        )

    def begin(which, t):
        part[which, t] = acc[...].reshape(part.shape[2:]).astype(jnp.bfloat16)
        for k in list(range(1, chips)) + [0]:
            near_copy(which, t, k).start()

    def fold(which, t):
        for k in range(1, chips):
            near_copy(which, t, k).wait_recv()
            away[which, t, k - 1] = (
                part[which, t, peer(k), core].astype(jnp.float32)
                + near[which, t, k].astype(jnp.float32)
            ).astype(jnp.bfloat16)
            far_copy(which, t, k).start()

    def ends(which):
        if which == 0:
            return section < sections - 1, section + 1, section > 0, section - 1
        return section > 0, section - 1, section < sections - 1, section + 1

    def finish(which, t):
        near_copy(which, t, 0).wait_recv()
        own = part[which, t, chip, core].astype(jnp.float32) + near[which, t, 0].astype(
            jnp.float32
        )
        for k in range(1, chips):
            far_copy(which, t, k).wait_recv()
            own = own + far[which, t, k - 1].astype(jnp.float32)
        before = cur[which, t, chip, core].astype(jnp.float32)
        if which == 0:
            result = before + own
        else:
            x = stash[t, chip, core].astype(jnp.float32)
            inverse = inverse_rms(x)
            cubed = inverse * inverse * inverse
            weighted = gain[...] * own
            result = (
                before
                + inverse * weighted
                - x * cubed * jnp.mean(x * weighted, axis=-1, keepdims=True)
            )
        share[which, t] = result.astype(jnp.bfloat16)
        sends, target, receives, _ = ends(which)

        if t == ticks - 1:
            cur[which, t + 1, chip, core] = result.astype(jnp.bfloat16)
            return

        @pl.when(sends)
        def _():
            lift_copy(which, t, target).start()

        @pl.when(jnp.logical_not(receives))
        def _():
            if which == 0:
                cur[which, t + 1, chip, core] = queue[order[t], chip, core]
            else:
                cur[which, t + 1, chip, core] = share[0, t]

    def spread(which, t):
        sends, target, receives, source = ends(which)

        if t < ticks - 1:
            @pl.when(receives)
            def _():
                lift_copy(which, t, source).wait_recv()

        for k in range(1, chips):
            gather_copy(which, t, k).start()
        pass_copy(which, t, 0).start()

    def relay(which, t):
        for k in range(1, chips):
            gather_copy(which, t, k).wait_recv()
            pass_copy(which, t, k).start()

    def settle(which, t):
        sends, target, receives, source = ends(which)
        relay(which, t)
        for k in range(chips):
            pass_copy(which, t, k).wait_recv()
        for k in range(chips):
            near_copy(which, t, k).wait_send()
            pass_copy(which, t, k).wait_send()
        for k in range(1, chips):
            far_copy(which, t, k).wait_send()
            gather_copy(which, t, k).wait_send()

        if t < ticks - 1:
            @pl.when(sends)
            def _():
                lift_copy(which, t, target).wait_send()

    stages = ((fold, 2), (finish, 4), (spread, 6))

    def normalize(place, x):
        normed[place * rows : (place + 1) * rows, :] = (
            x * inverse_rms(x) * gain[...]
        ).astype(jnp.bfloat16)

    def project(step, count):
        source = normed[: count * rows, :]
        return [mm(source, in_block(step, c), NN).astype(jnp.bfloat16) for c in range(3)]

    def advance(step, which, t):
        for stage, at in stages:
            @pl.when(step == at * steps // 8)
            def _(stage=stage):
                stage(which, t)

    def forward(t):
        def run(step, carry):
            if t > 0:
                advance(step, 1, t - 1)
            if t == 0:
                for c in range(3):
                    load(step, c).wait()
            qkv = project(step, 1 if t > 0 else ticks + 1)
            if t == 0:
                for c in range(3):
                    saved[step, c] = qkv[c][rows:]
            attended = []
            for h in range(pair):
                q, k, v = (a[:rows, h * head_dim : (h + 1) * head_dim] for a in qkv)
                probs = probabilities(q, k, bias[step * pair + h], scale).astype(jnp.bfloat16)
                attended.append(mm(probs, v, NN).astype(jnp.bfloat16))
            acc[...] += mm(jnp.concatenate(attended, axis=1), out_block(step), NN)
            return carry

        lax.fori_loop(0, steps, run, 0)

    def backward(t):
        def run(step, carry):
            advance(step, 0, t)
            grad_flat = mm(flat_down[...], out_block(step), NT).astype(jnp.bfloat16)
            stacked = []
            for h in range(pair):
                columns = slice(h * head_dim, (h + 1) * head_dim)
                q, k, v = (
                    saved[step, c, t * rows : (t + 1) * rows, columns] for c in range(3)
                )
                g = grad_flat[:, columns]
                probs = probabilities(q, k, bias[step * pair + h], scale)
                grad_probs = mm(g, v, NT)
                grad_value = mm(probs.astype(jnp.bfloat16), g, TN).astype(jnp.bfloat16)
                grad_scores = probs * (
                    grad_probs - jnp.sum(probs * grad_probs, axis=-1, keepdims=True)
                )
                half = grad_scores.astype(jnp.bfloat16)
                grad_query = (mm(half, k, NN) * scale).astype(jnp.bfloat16)
                grad_key = (mm(half, q, TN) * scale).astype(jnp.bfloat16)
                stacked.append((grad_query, grad_key, grad_value))
                if t == 0:
                    total[step * pair + h] = grad_scores
                else:
                    total[step * pair + h] += grad_scores
            back = [
                mm(jnp.concatenate(g, axis=1), in_block(step, c), NT)
                for c, g in enumerate(zip(*stacked))
            ]
            acc[...] += back[0] + back[1] + back[2]
            return carry

        lax.fori_loop(0, steps, run, 0)

    def tables(low, high):
        def run(b, carry):
            chosen = buckets[...] == b
            sums[b] = jnp.concatenate(
                [
                    jnp.sum(jnp.where(chosen, total[h], 0.0), axis=0, keepdims=True)
                    for h in range(total.shape[0])
                ],
                axis=0,
            )
            return carry

        lax.fori_loop(low, high, run, 0)

    for step in range(steps):
        for c in range(3):
            load(step, c).start()
    barrier = pltpu.get_barrier_semaphore()
    greeted = [twin] + [peer(k) * 2 + core for k in range(1, chips)]
    for other in greeted:
        pl.semaphore_signal(barrier, inc=1, device_id={"head": other}, device_id_type=MESH)

    @pl.when(section > 0)
    def _():
        pl.semaphore_signal(
            barrier, inc=1, device_id={"section": section - 1}, device_id_type=MESH
        )

    @pl.when(section < sections - 1)
    def _():
        pl.semaphore_signal(
            barrier, inc=1, device_id={"section": section + 1}, device_id_type=MESH
        )

    cur[0, 0] = rising[...]
    cur[1, 0] = falling[...]
    flat_down[...] = flat(falling[...]).astype(jnp.bfloat16)
    normalize(0, flat(rising[...]))
    for t in range(ticks):
        normalize(t + 1, flat(stash[t]))
    pl.semaphore_wait(
        barrier,
        len(greeted)
        + (section > 0).astype(jnp.int32)
        + (section < sections - 1).astype(jnp.int32),
    )
    for t in range(ticks):
        if t > 0:
            settle(0, t - 1)
            normalize(0, flat(cur[0, t]))
        acc[...] = jnp.zeros_like(acc)
        forward(t)
        begin(0, t)
        if t > 0:
            settle(1, t - 1)
            flat_down[...] = flat(cur[1, t]).astype(jnp.bfloat16)
        acc[...] = jnp.zeros_like(acc)
        backward(t)
        begin(1, t)
    last = ticks - 1
    settle(0, last)
    moved[0] = cur[0, ticks]
    count = sums.shape[0]
    for i, (stage, _at) in enumerate(stages):
        tables(i * count // 3, (i + 1) * count // 3)
        stage(1, last)
    table[...] = jnp.sum(sums[...], axis=-1)
    settle(1, last)
    moved[1] = cur[1, ticks]


def per_device(rising, falling, stash, queue, order, buckets, bias_table, gain, w_qkv, w_out):
    sections = lax.axis_size("section")
    head_count = lax.axis_size("head")
    ticks = stash.shape[1]
    rows, width = rising.shape[1:]
    heads, head_dim = w_qkv.shape[2], w_qkv.shape[4]
    chips, part_rows = head_count // 2, rows // head_count
    pair = next(p for p in (4, 4, 2, 1) if heads % p == 0)
    steps, span = heads // pair, pair * head_dim
    others = max(chips - 1, 1)
    w_in = jnp.swapaxes(w_qkv[0], 1, 2).reshape(width, 3 * heads * head_dim)
    w_back = w_out[0].reshape(heads * head_dim, width)
    bucket_ids = jnp.arange(bias_table.shape[1], dtype=jnp.int32)
    onehot = (buckets[None, :, :] == bucket_ids[:, None, None]).astype(jnp.float32)
    biases = jnp.einsum("bij,bh->hij", onehot, bias_table[0], precision=lax.Precision.HIGHEST)
    split = lambda a: a.reshape(a.shape[:-2] + (chips, 2, part_rows, width))
    vmem = pl.BlockSpec(memory_space=pltpu.VMEM)
    tile = (part_rows, width)
    bf16 = lambda *shape: pltpu.VMEM(shape, jnp.bfloat16)
    dma = lambda *shape: pltpu.SemaphoreType.DMA(shape)
    moved, table = pl.pallas_call(
        functools.partial(wave_kernel, ticks, steps, pair, head_dim, chips, sections),
        in_specs=[pl.BlockSpec(memory_space=pltpu.SMEM)] + [vmem] * 7 + [pl.BlockSpec(memory_space=pl.ANY), vmem],
        out_specs=[vmem] * 2,
        out_shape=[
            jax.ShapeDtypeStruct((2, chips, 2) + tile, jnp.bfloat16),
            jax.ShapeDtypeStruct((bias_table.shape[1], heads), jnp.float32),
        ],
        scratch_shapes=[
            bf16(steps, 3, width, span),
            dma(steps, 3),
            bf16((ticks + 1) * rows, width),
            bf16(steps, 3, ticks * rows, span),
            bf16(rows, width),
            pltpu.VMEM((rows, width), jnp.float32),
            pltpu.VMEM((heads, rows, rows), jnp.float32),
            pltpu.VMEM((bias_table.shape[1], heads, rows), jnp.float32),
            bf16(2, ticks + 1, chips, 2, *tile),
            bf16(2, ticks, chips, 2, *tile),
            bf16(2, ticks, chips, *tile),
            bf16(2, ticks, others, *tile),
            bf16(2, ticks, others, *tile),
            bf16(2, ticks, *tile),
            dma(2, ticks, chips), dma(2, ticks, chips),
            dma(2, ticks, others), dma(2, ticks, others),
            dma(2, ticks), dma(2, ticks),
            dma(2, ticks, others), dma(2, ticks, others),
            dma(2, ticks, chips), dma(2, ticks, chips),
        ],
        compiler_params=pltpu.CompilerParams(
            collective_id=0, has_side_effects=True, vmem_limit_bytes=40 << 20
        ),
    )(
        order, split(rising[0]), split(falling[0]), split(stash[0]), split(queue), gain,
        biases, buckets, w_in, w_back,
    )
    moved = moved.reshape(2, 1, rows, width)
    return (moved[0], moved[1], table[None])


def solution(mesh):
    return jax.shard_map(
        per_device,
        mesh=mesh,
        in_specs=(
            P(("groups", "section"), None, None),
            P(("groups", "section"), None, None),
            P(("groups", "section"), None, None, None),
            P("groups", None, None),
            P("groups"),
            P(),
            P("section", None, "head"),
            P("section", None),
            P("section", None, "head", None, None),
            P("section", "head", None, None),
        ),
        out_specs=(
            P(("groups", "section"), None, None),
            P(("groups", "section"), None, None),
            P(("groups", "section"), None, "head"),
        ),
        check_vma=False,
    )
```
